256 devices in a mesh: tm: 8 (over y, core), head: 32 (over z, x).
Axes of the slice: x: 4, y: 4, z: 8, core: 2. Of those that a mesh axis runs over, the one named last changes fastest.
Arguments:
- tokens: bfloat16 [4096, 5120], P('tm'), may hold values from -24 to 24
- w_query: bfloat16 [5120, 4096], P(None, 'head'), may hold values from -0.078125 to 0.078125
- w_key: bfloat16 [5120, 4096], P(None, 'head'), may hold values from -0.078125 to 0.078125
- w_value: bfloat16 [5120, 4096], P(None, 'head'), may hold values from -0.078125 to 0.078125
- w_out: bfloat16 [4096, 5120], P('head'), may hold values from -0.09375 to 0.09375
- out_grad: bfloat16 [4096, 5120], P('tm'), may hold values from -6 to 6
- frame_lists: int32 [8, 8], replicated, may hold values from 0 to 1, as said below
Outputs:
- token_grad: bfloat16 [4096, 5120], P(('tm', 'head'))
- query_grad: bfloat16 [5120, 4096], P('tm', 'head')
- key_grad: bfloat16 [5120, 4096], P('tm', 'head')
- value_grad: bfloat16 [5120, 4096], P('tm', 'head')
- out_weight_grad: bfloat16 [4096, 5120], P('head', 'tm')
The draws below stay inside these ranges and needn't reach their ends.
Inputs may be any that keep to these rules, and one draw needn't show every extreme that they name: `frame_lists`: entries with j >= i are 0; entry (i, i - 1) is 1 for every group i > 0.
All inputs are finite; a program needn't handle non-finite values.
Results may differ from the reference program's by a relative error of at most 0.02.
The reference program's roundings to bfloat16 on the way (of `d_attn`, `attn` and `dscore`) count: a program that leaves them out, or rounds other values in their place, can miss the bound.
Values may be sent and summed in bfloat16 or wider, within the bound.
A program may use at most 128 MiB of HBM per device.

```python
import jax
import jax.numpy as jnp
from jax import lax

D = 5120
HD = 128
GROUP = 512
HEADS = 32
GROUPS = 8
TOKENS = 4096


def draw_tokens(key, part):
    first = jax.random.fold_in(key, 11)
    base = jax.random.normal(first, (TOKENS, D), jnp.float32)
    return jnp.clip(base, -6.0, 6.0).astype(jnp.bfloat16)


def draw_frame_lists(key, part):
    bits = jax.random.randint(jax.random.fold_in(key, 21), (GROUPS, GROUPS), 0, 2, jnp.int32)
    rowid = jnp.arange(GROUPS, dtype=jnp.int32)[:, None]
    colid = jnp.arange(GROUPS, dtype=jnp.int32)[None, :]
    lower = jnp.where(colid < rowid, bits, 0)
    return jnp.where(colid == rowid - 1, 1, lower).astype(jnp.int32)


def level_of(rng, extent, pieces, low, high):
    gain = 1.0
    for axis_at, parts in pieces:
        draws = jax.random.uniform(jax.random.fold_in(jax.random.fold_in(rng, 6), axis_at), (parts,), jnp.float32, low / len(pieces), high / len(pieces))
        gain = gain * jnp.repeat(jnp.exp(draws), extent[axis_at] // parts).reshape((-1,) + (1,) * (len(extent) - 1 - axis_at))
    return gain


def bell_draw(own_key, extent, spread, reach, split=(), held_as=jnp.bfloat16):
    result = jax.random.normal(own_key, extent, jnp.float32) * spread
    if len(split) > 0:
        result = level_of(own_key, extent, split, -0.22, 0.18) * result
    return jnp.clip(result, min=-reach, max=reach).astype(held_as)


def setup_inputs(seed: int = 0) -> dict:
    streams_of = jax.random.split(jax.random.key(seed), 8)
    tokens = draw_tokens(jax.random.fold_in(streams_of[7], 71), 0)
    w_query = bell_draw(streams_of[1], (D, HEADS * HD), D ** -0.5, 0.078125, ((1, 32),))
    w_key = bell_draw(streams_of[2], (D, HEADS * HD), D ** -0.5, 0.078125, ((1, 32),))
    w_value = bell_draw(streams_of[3], (D, HEADS * HD), D ** -0.5, 0.078125, ((1, 32),))
    w_out = bell_draw(streams_of[4], (HEADS * HD, D), (HEADS * HD) ** -0.5, 0.09375, ((0, 32),))
    out_grad = bell_draw(streams_of[5], (TOKENS, D), 1.0, 6.0, ((0, 8),))
    frame_lists = draw_frame_lists(jax.random.fold_in(streams_of[7], 71), 0)
    return dict(tokens=tokens, w_query=w_query, w_key=w_key, w_value=w_value, w_out=w_out, out_grad=out_grad, frame_lists=frame_lists)


def round_keep(value):
    return lax.optimization_barrier(value.astype(jnp.bfloat16)).astype(jnp.float32)


def reference(tokens, w_query, w_key, w_value, w_out, out_grad, frame_lists):
    heads = w_query.shape[1] // HD
    scale = 1.0 / (HD ** 0.5)
    query = jnp.dot(tokens, w_query, preferred_element_type=jnp.float32).astype(jnp.bfloat16)
    keys = jnp.dot(tokens, w_key, preferred_element_type=jnp.float32).astype(jnp.bfloat16)
    values = jnp.dot(tokens, w_value, preferred_element_type=jnp.float32).astype(jnp.bfloat16)
    d_attn = jnp.dot(out_grad, w_out.T, preferred_element_type=jnp.float32).astype(jnp.bfloat16)
    count = frame_lists.shape[0]
    rowid = jnp.arange(count)[:, None]
    colid = jnp.arange(count)[None, :]
    allowed = (rowid == colid) | ((frame_lists == 1) & (colid < rowid))
    group_of = jnp.arange(TOKENS) // GROUP
    token_mask = allowed[group_of][:, group_of]

    def one_head(index):
        start = (index * HD).astype(jnp.int32)
        qh = lax.dynamic_slice_in_dim(query, start, HD, 1)
        kh = lax.dynamic_slice_in_dim(keys, start, HD, 1)
        vh = lax.dynamic_slice_in_dim(values, start, HD, 1)
        gh = lax.dynamic_slice_in_dim(d_attn, start, HD, 1)
        scores = jnp.dot(qh, kh.T, preferred_element_type=jnp.float32) * scale
        scores = jnp.where(token_mask, scores, jnp.float32(-1e30))
        top = jnp.max(scores, axis=1, keepdims=True)
        expd = jnp.exp(scores - top)
        probs = expd / jnp.sum(expd, axis=1, keepdims=True)
        probs_b = probs.astype(jnp.bfloat16)
        attn = jnp.dot(probs_b, vh, preferred_element_type=jnp.float32).astype(jnp.bfloat16)
        dprobs = jnp.dot(gh, vh.T, preferred_element_type=jnp.float32)
        delta = jnp.sum(probs * dprobs, axis=1, keepdims=True)
        dscore = (probs * (dprobs - delta) * scale).astype(jnp.bfloat16)
        dq = jnp.dot(dscore, kh, preferred_element_type=jnp.float32).astype(jnp.bfloat16)
        dk = jnp.dot(dscore.T, qh, preferred_element_type=jnp.float32).astype(jnp.bfloat16)
        dv = jnp.dot(probs_b.T, gh, preferred_element_type=jnp.float32).astype(jnp.bfloat16)
        return attn, dq, dk, dv

    stacked = lax.map(one_head, jnp.arange(heads, dtype=jnp.int32))

    def flatten(block):
        return jnp.transpose(block, (1, 0, 2)).reshape(TOKENS, heads * HD)

    attn, dquery, dkey, dvalue = [flatten(block) for block in stacked]
    token_grad = (jnp.dot(dquery, w_query.T, preferred_element_type=jnp.float32)
                  + jnp.dot(dkey, w_key.T, preferred_element_type=jnp.float32)
                  + jnp.dot(dvalue, w_value.T, preferred_element_type=jnp.float32)).astype(jnp.bfloat16)
    grad_q = jnp.zeros((D, heads * HD), jnp.float32)
    grad_k = jnp.zeros((D, heads * HD), jnp.float32)
    grad_v = jnp.zeros((D, heads * HD), jnp.float32)
    grad_o = jnp.zeros((heads * HD, D), jnp.float32)
    for group in range(GROUPS):
        lower = group * GROUP
        upper = lower + GROUP
        xpart = tokens[lower:upper]
        grad_q = grad_q + round_keep(jnp.dot(xpart.T, dquery[lower:upper], preferred_element_type=jnp.float32))
        grad_k = grad_k + round_keep(jnp.dot(xpart.T, dkey[lower:upper], preferred_element_type=jnp.float32))
        grad_v = grad_v + round_keep(jnp.dot(xpart.T, dvalue[lower:upper], preferred_element_type=jnp.float32))
        grad_o = grad_o + round_keep(jnp.dot(attn[lower:upper].T, out_grad[lower:upper], preferred_element_type=jnp.float32))
    return (token_grad, grad_q.astype(jnp.bfloat16), grad_k.astype(jnp.bfloat16),
            grad_v.astype(jnp.bfloat16), grad_o.astype(jnp.bfloat16))
```

```python
import functools

import jax
import jax.numpy as jnp
from jax import lax
from jax.experimental import pallas as pl
from jax.experimental.pallas import tpu as pltpu
from jax.sharding import PartitionSpec as P

MESH = pl.DeviceIdType.MESH
BF = jnp.bfloat16
F32 = jnp.float32
CHUNKS = (("x", 1024), ("z", 1024), ("x", 1024), ("z", 1024), ("x", 1024))
NX, NY, NZ = 4, 4, 8


def dot_nt(left, right):
    return lax.dot_general(left, right, (((1,), (1,)), ((), ())), preferred_element_type=F32)


def place():
    t, h = lax.axis_index("tm"), lax.axis_index("head")
    return lax.div(t, 2), lax.rem(t, 2), lax.div(h, NX), lax.rem(h, NX)


def device(y, c, z, x):
    return (y * 2 + c, z * NX + x)


def turn(at, by, n):
    return lax.rem(at + by + n, n)


def peer_on(axis, step):
    y, c, z, x = place()
    if axis == "x":
        return device(y, c, z, turn(x, step, NX))
    if axis == "y":
        return device(turn(y, step, NY), c, z, x)
    if axis == "z":
        return device(y, c, turn(z, step, NZ), x)
    return device(y, 1 - c, z, x)


class Ring:
    def __init__(self, axis, n, me, own, land, sems, base):
        self.axis, self.n, self.me, self.own, self.land = axis, n, me, own, land
        self.send, self.recv = sems
        self.ids, count = {}, 0
        for p in range(n // 2):
            for way, half in ((0, 0), (1, 1), (0, 1), (1, 0)):
                if p < self.length(way, half):
                    self.ids[way, half, p] = count
                    count += 1
        self.base = base
        self.count = count

    def length(self, way, half):
        return self.n // 2 if way == half else self.n // 2 - 1

    def copy(self, way, half, p):
        step = (-1, 1)[way]
        target = turn(self.me, step * (self.length(way, half) - p), self.n)
        i = self.ids[way, half, p]
        return target, pltpu.make_async_remote_copy(
            src_ref=self.own(target, half),
            dst_ref=self.land.at[i],
            send_sem=self.send.at[self.base + i],
            recv_sem=self.recv.at[self.base + i],
            device_id=peer_on(self.axis, step),
            device_id_type=MESH,
        )

    def step(self, p):
        for way, half in ((0, 0), (1, 1), (0, 1), (1, 0)):
            if p >= self.length(way, half):
                continue
            target, copy = self.copy(way, half, p)
            if p > 0:
                self.copy(way, half, p - 1)[1].wait_recv()
                mine = self.own(target, half)
                mine[...] = mine[...] + self.land[self.ids[way, half, p - 1]]
            copy.start()

    def finish(self, write):
        for half in (0, 1):
            total = self.own(self.me, half)[...].astype(F32)
            for way in (0, 1):
                last = self.length(way, half) - 1
                self.copy(way, half, last)[1].wait_recv()
                total = total + self.land[self.ids[way, half, last]].astype(F32)
            write(half, total)

    def drain(self):
        for way, half, p in self.ids:
            self.copy(way, half, p)[1].wait_send()


def greet(axes):
    barrier = pltpu.get_barrier_semaphore()
    peers = []
    for axis in axes:
        peers += [peer_on(axis, 1)] if axis == "c" else [peer_on(axis, -1), peer_on(axis, 1)]
    for peer in peers:
        pl.semaphore_signal(barrier, inc=1, device_id=peer, device_id_type=MESH)
    pl.semaphore_wait(barrier, len(peers))


def grads_kernel(
    tokens_hbm, outg_hbm, wk_hbm, wv_hbm, wq_hbm, d_ref, dt_ref, at_ref,
    tg_ref, qg_ref, kg_ref, vg_ref, og_ref,
    tokens, outg, wcat, wp, pair_land, y_land, in_sem, send_sem, recv_sem, *bufs
):
    y, c, z, x = place()
    sems = (send_sem, recv_sem)
    loads = [
        pltpu.make_async_copy(src, wcat.at[:, pl.ds(i * 128, 128)], in_sem.at[i])
        for i, src in enumerate((wk_hbm, wv_hbm, wq_hbm))
    ]
    loads += [
        pltpu.make_async_copy(tokens_hbm, tokens, in_sem.at[3]),
        pltpu.make_async_copy(outg_hbm, outg, in_sem.at[4]),
    ]
    for load in loads:
        load.start()

    base = 10
    chunks = []
    offset = 0
    for n, (kind, width) in enumerate(CHUNKS):
        part, land1, mid, land2 = bufs[4 * n : 4 * n + 4]
        wide = width // 2
        if kind == "x":
            first = Ring("x", NX, x, lambda b, h, part=part: part.at[pl.ds(h * 4, 4), b], land1, sems, base)
            second = Ring(
                "z", NZ, z, lambda b, h, mid=mid, wide=wide: mid.at[b, :, pl.ds(h * wide, wide)],
                land2, sems, base + first.count,
            )
        else:
            first = Ring("z", NZ, z, lambda b, h, part=part: part.at[b, pl.ds(h * 2, 2)], land1, sems, base)
            second = Ring(
                "x", NX, x, lambda b, h, mid=mid, wide=wide: mid.at[b, :, pl.ds(h * wide, wide)],
                land2, sems, base + first.count,
            )
        base += first.count + second.count
        chunks.append((kind, width, offset, part, mid, first, second))
        offset += width

    def token_part(n):
        kind, width, at, part, mid, first, second = chunks[n]

        def piece(i, _):
            cols = pl.multiple_of(i * 256, 256)
            got = dot_nt(d_ref[...], wcat[pl.ds(pl.multiple_of(at + cols, 256), 256), :])
            part[:, :, :, pl.ds(cols, 256)] = got.astype(BF).reshape(NZ, NX, 16, 256)
            return 0

        lax.fori_loop(0, width // 256, piece, 0)

    def middle(n):
        kind, width, at, part, mid, first, second = chunks[n]
        count = 4 if kind == "x" else 2

        def write(half, total):
            mid[pl.ds(half * count, count)] = total.astype(BF)

        first.finish(write)

    def end(n):
        kind, width, at, part, mid, first, second = chunks[n]

        def write(half, total):
            tg_ref[:, pl.ds(at + half * (width // 2), width // 2)] = total.astype(BF)

        second.finish(write)

    def weight_block(yt, ct):
        cols = pl.ds(pl.multiple_of((yt * 2 + ct) * 640, 128), 640)
        top = jnp.dot(dt_ref[...], tokens[:, cols], preferred_element_type=F32)
        low = jnp.dot(at_ref[...], outg[:, cols], preferred_element_type=F32)
        return top, low

    def pair_copy(j):
        yt = turn(y, 2 + 3 * j, NY)
        return yt, pltpu.make_async_remote_copy(
            src_ref=wp.at[yt, 1 - c], dst_ref=pair_land.at[yt],
            send_sem=send_sem.at[j], recv_sem=recv_sem.at[j],
            device_id=peer_on("c", 1), device_id_type=MESH,
        )

    def theirs(j, _):
        yt, copy = pair_copy(j)
        top, low = weight_block(yt, 1 - c)
        wp[yt, 1 - c, 0:384, :] = top.astype(BF)
        wp[yt, 1 - c, 384:512, :] = low.astype(BF)
        copy.start()
        return 0

    def ours(j, _):
        yt, copy = pair_copy(j)
        top, low = weight_block(yt, c)
        copy.wait_recv()
        wp[yt, c, 0:384, :] = (top + pair_land[yt, 0:384, :].astype(F32)).astype(BF)
        wp[yt, c, 384:512, :] = (low + pair_land[yt, 384:512, :].astype(F32)).astype(BF)
        return 0

    yring = Ring("y", NY, y, lambda b, h: wp.at[b, c, pl.ds(h * 256, 256)], y_land, sems, 4)

    greet(("x", "z", "y", "c"))
    for load in loads[:3]:
        load.wait()
    firsts = [chunk[5] for chunk in chunks]
    seconds = [chunk[6] for chunk in chunks]
    token_part(0)
    firsts[0].step(0)
    token_part(1)
    firsts[1].step(0)
    loads[3].wait()
    loads[4].wait()
    lax.fori_loop(0, 4, theirs, 0)
    token_part(2)
    firsts[2].step(0)
    token_part(3)
    firsts[3].step(0)
    lax.fori_loop(0, 4, ours, 0)
    yring.step(0)
    firsts[0].step(1)
    token_part(4)
    firsts[1].step(1)
    firsts[4].step(0)
    firsts[3].step(1)
    firsts[2].step(1)
    yring.step(1)
    firsts[1].step(2)
    middle(0)
    seconds[0].step(0)
    firsts[3].step(2)
    firsts[4].step(1)
    seconds[0].step(1)
    firsts[1].step(3)
    seconds[0].step(2)
    firsts[3].step(3)
    middle(2)
    seconds[2].step(0)
    seconds[0].step(3)
    middle(1)
    seconds[1].step(0)
    seconds[2].step(1)
    middle(3)
    seconds[3].step(0)
    middle(4)
    seconds[4].step(0)
    seconds[1].step(1)
    seconds[2].step(2)
    seconds[4].step(1)
    seconds[3].step(1)
    seconds[2].step(3)
    seconds[4].step(2)
    end(0)
    end(1)

    def weights_out(half, total):
        if half == 0:
            kg_ref[...] = total[0:128].T.astype(BF)
            vg_ref[...] = total[128:256].T.astype(BF)
        else:
            qg_ref[...] = total[0:128].T.astype(BF)
            og_ref[...] = total[128:256].astype(BF)

    yring.finish(weights_out)
    seconds[4].step(3)
    end(3)
    end(2)
    end(4)
    for j in range(4):
        pair_copy(j)[1].wait_send()
    yring.drain()
    for ring in firsts + seconds:
        ring.drain()


def grads(tokens, out_grad, wk, wv, wq, d, dt, at):
    bufs = []
    for kind, width in CHUNKS:
        bufs.append(pltpu.VMEM((NZ, NX, 16, width), BF))
        if kind == "x":
            bufs += [
                pltpu.VMEM((6, 4, 16, width), BF), pltpu.VMEM((NZ, 16, width), BF),
                pltpu.VMEM((14, 16, width // 2), BF),
            ]
        else:
            bufs += [
                pltpu.VMEM((14, 2, 16, width), BF), pltpu.VMEM((NX, 16, width), BF),
                pltpu.VMEM((6, 16, width // 2), BF),
            ]
    count = 10 + 20 * len(CHUNKS)
    hbm = pl.BlockSpec(memory_space=pl.ANY)
    vmem = pl.BlockSpec(memory_space=pltpu.VMEM)
    return pl.pallas_call(
        grads_kernel,
        out_shape=(
            jax.ShapeDtypeStruct((16, 5120), BF),
            jax.ShapeDtypeStruct((640, 128), BF),
            jax.ShapeDtypeStruct((640, 128), BF),
            jax.ShapeDtypeStruct((640, 128), BF),
            jax.ShapeDtypeStruct((128, 640), BF),
        ),
        in_specs=[hbm] * 5 + [vmem] * 3,
        out_specs=[vmem] * 5,
        scratch_shapes=[
            pltpu.VMEM((512, 5120), BF),
            pltpu.VMEM((512, 5120), BF),
            pltpu.VMEM((5120, 384), BF),
            pltpu.VMEM((NY, 2, 512, 640), BF),
            pltpu.VMEM((NY, 512, 640), BF),
            pltpu.VMEM((6, 256, 640), BF),
            pltpu.SemaphoreType.DMA((5,)),
            pltpu.SemaphoreType.DMA((count,)),
            pltpu.SemaphoreType.DMA((count,)),
        ] + bufs,
        compiler_params=pltpu.CompilerParams(
            collective_id=1, has_side_effects=True, vmem_limit_bytes=62 * 2**20
        ),
    )(tokens, out_grad, wk, wv, wq, d, dt, at)


def contract_rows(left, right):
    return lax.dot_general(
        left, right, (((0,), (0,)), ((), ())), preferred_element_type=jnp.float32
    )


def contract_cols(left, right):
    return lax.dot_general(
        left, right, (((1,), (1,)), ((), ())), preferred_element_type=jnp.float32
    )


def local(tokens, w_query, w_key, w_value, w_out, out_grad, frame_lists):
    width = w_query.shape[1]
    scale = 1.0 / width**0.5
    rows = tokens.shape[0]
    groups = lax.axis_size("tm")
    mine = lax.axis_index("tm")
    query = jnp.dot(tokens, w_query, preferred_element_type=jnp.float32).astype(jnp.bfloat16)
    keys = jnp.dot(tokens, w_key, preferred_element_type=jnp.float32).astype(jnp.bfloat16)
    values = jnp.dot(tokens, w_value, preferred_element_type=jnp.float32).astype(jnp.bfloat16)
    d_attn = contract_cols(out_grad, w_out).astype(jnp.bfloat16)
    my_list = lax.dynamic_slice_in_dim(frame_lists, mine, 1, 0)[0]
    key_all, value_all = (
        lax.all_gather(keys, "tm", axis=0, tiled=True),
        lax.all_gather(values, "tm", axis=0, tiled=True),
    )
    order = jnp.arange(groups, dtype=jnp.int32)
    allowed = (order == mine) | (my_list == 1) & (order < mine)
    key_mask = jnp.repeat(allowed, rows)[None, :]
    scores = contract_cols(query, key_all) * scale
    scores = jnp.where(key_mask, scores, jnp.float32(-1e30))
    top = jnp.max(scores, axis=1, keepdims=True)
    expd = jnp.exp(scores - top)
    probs = expd / jnp.sum(expd, axis=1, keepdims=True)
    probs_b = probs.astype(jnp.bfloat16)
    attn = jnp.dot(probs_b, value_all, preferred_element_type=jnp.float32).astype(jnp.bfloat16)
    dprobs = contract_cols(d_attn, value_all)
    delta = jnp.sum(probs * dprobs, axis=1, keepdims=True)
    dscore = (probs * (dprobs - delta) * scale).astype(jnp.bfloat16)
    dquery = jnp.dot(dscore, key_all, preferred_element_type=jnp.float32).astype(jnp.bfloat16)
    cache_terms = jnp.concatenate(
        [contract_rows(dscore, query), contract_rows(probs_b, d_attn)], axis=1
    )
    summed = lax.psum_scatter(
        cache_terms.astype(jnp.bfloat16), "tm", scatter_dimension=0, tiled=True
    ).astype(jnp.float32)
    dkey = summed[:, :width].astype(jnp.bfloat16)
    dvalue = summed[:, width:].astype(jnp.bfloat16)
    d = jnp.concatenate([dkey, dvalue, dquery], axis=1)
    return grads(tokens, out_grad, w_key, w_value, w_query, d, d.T, attn.T)


def solution(mesh):
    in_specs = (
        P("tm", None),
        P(None, "head"),
        P(None, "head"),
        P(None, "head"),
        P("head", None),
        P("tm", None),
        P(),
    )
    out_specs = (
        P(("tm", "head"), None),
        P("tm", "head"),
        P("tm", "head"),
        P("tm", "head"),
        P("head", "tm"),
    )
    return jax.shard_map(local, mesh=mesh, in_specs=in_specs, out_specs=out_specs, check_vma=False)
```

```python
import jax
import jax.numpy as jnp
from jax import lax
from jax.experimental import pallas as pl
from jax.experimental.pallas import tpu as pltpu
from jax.sharding import PartitionSpec as P

MESH = pl.DeviceIdType.MESH
BF = jnp.bfloat16
F32 = jnp.float32
CHUNKS = (("x", 1024), ("z", 1024), ("x", 1024), ("z", 1024), ("x", 1024))
NX, NY, NZ = 4, 4, 8
GATHER = 10 + 20 * len(CHUNKS)


def dot_nt(left, right):
    return lax.dot_general(left, right, (((1,), (1,)), ((), ())), preferred_element_type=F32)


def dot_tn(left, right):
    return lax.dot_general(left, right, (((0,), (0,)), ((), ())), preferred_element_type=F32)


def place():
    t, h = lax.axis_index("tm"), lax.axis_index("head")
    return lax.div(t, 2), lax.rem(t, 2), lax.div(h, NX), lax.rem(h, NX)


def device(y, c, z, x):
    return (y * 2 + c, z * NX + x)


def turn(at, by, n):
    return lax.rem(at + by + n, n)


def peer_on(axis, step):
    y, c, z, x = place()
    if axis == "x":
        return device(y, c, z, turn(x, step, NX))
    if axis == "y":
        return device(turn(y, step, NY), c, z, x)
    if axis == "z":
        return device(y, c, turn(z, step, NZ), x)
    return device(y, 1 - c, z, x)


class Ring:
    def __init__(self, axis, n, me, own, land, sems, base):
        self.axis, self.n, self.me, self.own, self.land = axis, n, me, own, land
        self.send, self.recv = sems
        self.ids, count = {}, 0
        for p in range(n // 2):
            for way, half in ((0, 0), (1, 1), (0, 1), (1, 0)):
                if p < self.length(way, half):
                    self.ids[way, half, p] = count
                    count += 1
        self.base = base
        self.count = count

    def length(self, way, half):
        return self.n // 2 if way == half else self.n // 2 - 1

    def copy(self, way, half, p):
        step = (-1, 1)[way]
        target = turn(self.me, step * (self.length(way, half) - p), self.n)
        i = self.ids[way, half, p]
        return target, pltpu.make_async_remote_copy(
            src_ref=self.own(target, half),
            dst_ref=self.land.at[i],
            send_sem=self.send.at[self.base + i],
            recv_sem=self.recv.at[self.base + i],
            device_id=peer_on(self.axis, step),
            device_id_type=MESH,
        )

    def step(self, p):
        for way, half in ((0, 0), (1, 1), (0, 1), (1, 0)):
            if p >= self.length(way, half):
                continue
            target, copy = self.copy(way, half, p)
            if p > 0:
                self.copy(way, half, p - 1)[1].wait_recv()
                mine = self.own(target, half)
                mine[...] = mine[...] + self.land[self.ids[way, half, p - 1]]
            copy.start()

    def finish(self, write):
        for half in (0, 1):
            total = self.own(self.me, half)[...].astype(F32)
            for way in (0, 1):
                last = self.length(way, half) - 1
                self.copy(way, half, last)[1].wait_recv()
                total = total + self.land[self.ids[way, half, last]].astype(F32)
            write(half, total)

    def drain(self):
        for way, half, p in self.ids:
            self.copy(way, half, p)[1].wait_send()


def greet(axes):
    barrier = pltpu.get_barrier_semaphore()
    peers = []
    for axis in axes:
        peers += [peer_on(axis, 1)] if axis == "c" else [peer_on(axis, -1), peer_on(axis, 1)]
    for peer in peers:
        pl.semaphore_signal(barrier, inc=1, device_id=peer, device_id_type=MESH)
    pl.semaphore_wait(barrier, len(peers))


def grads_kernel(
    tokens_hbm, outg_hbm, wk_hbm, wv_hbm, wq_hbm, wo_hbm, lists_ref,
    tg_ref, qg_ref, kg_ref, vg_ref, og_ref,
    tokens, outg, wcat, wout, kv, query, d_attn, scores, dprobs, top_ref, sum_ref, del_ref, atf, dqf,
    cache, cache_pair, cache_land, d_ref, dt_ref, at_ref,
    wp, pair_land, y_land, in_sem, send_sem, recv_sem, *bufs
):
    y, c, z, x = place()
    sems = (send_sem, recv_sem)
    me = y * 2 + c
    scale = 1.0 / 128**0.5
    loads = [
        pltpu.make_async_copy(src, dst, in_sem.at[i])
        for i, (src, dst) in enumerate((
            (wk_hbm, wcat.at[:, pl.ds(0, 128)]), (wv_hbm, wcat.at[:, pl.ds(128, 128)]), (tokens_hbm, tokens),
            (wq_hbm, wcat.at[:, pl.ds(256, 128)]), (outg_hbm, outg), (wo_hbm, wout),
        ))
    ]
    for load in loads:
        load.start()

    def block(dy, core):
        return turn(y, dy, NY) * 2 + core

    def move(i, blk, rows, axis, step):
        ref = kv.at[blk, rows]
        return pltpu.make_async_remote_copy(
            src_ref=ref, dst_ref=ref,
            send_sem=send_sem.at[GATHER + i], recv_sem=recv_sem.at[GATHER + i],
            device_id=peer_on(axis, step), device_id_type=MESH,
        )

    low, high, whole = pl.ds(0, 256), pl.ds(256, 256), pl.ds(0, 512)
    near = [
        move(0, me, low, "y", 1), move(3, me, high, "y", -1),
        move(1, me, high, "y", 1), move(2, me, low, "y", -1),
    ]
    far = [move(4, block(3, c), low, "y", 1), move(5, block(1, c), high, "y", -1)]
    across = [move(6 + dy, block(dy, c), whole, "c", 1) for dy in range(4)]

    def span(k):
        return pl.ds(pl.multiple_of(k * 640, 128), 640)

    def project_kv(k, _):
        scores[0, :, 0:256] += jnp.dot(tokens[:, span(k)], wcat[span(k), 0:256], preferred_element_type=F32)
        return 0

    def project_rest(k, _):
        scores[0, :, 0:128] += jnp.dot(tokens[:, span(k)], wcat[span(k), 256:384], preferred_element_type=F32)
        scores[0, :, 128:256] += dot_nt(outg[:, span(k)], wout[:, span(k)])
        return 0

    greet(("x", "z", "y", "c"))
    scores[0] = jnp.zeros((512, 512), F32)
    for load in loads[:3]:
        load.wait()
    lax.fori_loop(0, 8, project_kv, 0)
    kv[me] = scores[0, :, 0:256].astype(BF)
    for copy in near:
        copy.start()
    across[0].start()
    scores[0] = jnp.zeros((512, 512), F32)
    for load in loads[3:]:
        load.wait()
    lax.fori_loop(0, 8, project_rest, 0)
    query[...] = scores[0, :, 0:128].astype(BF)
    d_attn[...] = scores[0, :, 128:256].astype(BF)
    top_ref[...] = jnp.full((1, 512), -3e30, F32)
    sum_ref[...] = jnp.zeros((1, 512), F32)
    del_ref[...] = jnp.zeros((1, 512), F32)
    atf[...] = jnp.zeros((128, 512), F32)
    dqf[...] = jnp.zeros((128, 512), F32)

    def score(i, _):
        pair, other = lax.div(i, 2), lax.rem(i, 2)
        dy = jnp.where(pair == 1, 3, jnp.where(pair == 2, 1, jnp.where(pair == 3, 2, 0)))
        b = block(dy, jnp.where(other == 1, 1 - c, c))

        @pl.when(i == 1)
        def _():
            across[0].wait_recv()

        @pl.when(i == 2)
        def _():
            near[0].wait_recv()
            far[0].start()
            near[1].wait_recv()
            far[1].start()
            near[2].wait_recv()
            across[3].start()
            near[3].wait_recv()
            across[1].start()

        @pl.when(i == 3)
        def _():
            across[3].wait_recv()

        @pl.when(i == 5)
        def _():
            across[1].wait_recv()

        @pl.when(i == 6)
        def _():
            far[0].wait_recv()
            far[1].wait_recv()
            across[2].start()

        @pl.when(i == 7)
        def _():
            across[2].wait_recv()

        seen = (b == me) | ((b < me) & (lists_ref[me, b] == 1))
        shut = jnp.where(seen, 0.0, -1e30).astype(F32)
        got = dot_nt(kv[b, :, 0:128], query[...]) * scale + shut
        scores[b] = got
        top_ref[...] = jnp.maximum(top_ref[...], jnp.max(got, axis=0, keepdims=True))
        dprobs[b] = dot_nt(kv[b, :, 128:256], d_attn[...])
        return 0

    lax.fori_loop(0, 8, score, 0)

    def weigh(b, _):
        got = jnp.exp(scores[b] - top_ref[...])
        scores[b] = got
        sum_ref[...] += jnp.sum(got, axis=0, keepdims=True)
        del_ref[...] += jnp.sum(got * dprobs[b], axis=0, keepdims=True)
        return 0

    lax.fori_loop(0, 8, weigh, 0)
    sum_ref[...] = 1.0 / sum_ref[...]
    del_ref[...] = del_ref[...] * sum_ref[...]

    def cache_block(b):
        probs = scores[b] * sum_ref[...]
        probs_b = probs.astype(BF)
        dscore = (probs * (dprobs[b] - del_ref[...]) * scale).astype(BF)
        atf[...] += dot_tn(kv[b, :, 128:256], probs_b)
        dqf[...] += dot_tn(kv[b, :, 0:128], dscore)
        dk = jnp.dot(dscore, query[...], preferred_element_type=F32)
        dv = jnp.dot(probs_b, d_attn[...], preferred_element_type=F32)
        return dk, dv

    def cache_copy(j):
        yt = turn(y, 2 + 3 * j, NY)
        return yt, pltpu.make_async_remote_copy(
            src_ref=cache.at[yt, 1 - c], dst_ref=cache_pair.at[yt],
            send_sem=send_sem.at[GATHER + 10 + j], recv_sem=recv_sem.at[GATHER + 10 + j],
            device_id=peer_on("c", 1), device_id_type=MESH,
        )

    def cache_theirs(j, _):
        yt, copy = cache_copy(j)
        dk, dv = cache_block(yt * 2 + 1 - c)
        cache[yt, 1 - c, :, 0:128] = dk.astype(BF)
        cache[yt, 1 - c, :, 128:256] = dv.astype(BF)
        copy.start()
        return 0

    def cache_ours(j, _):
        yt, copy = cache_copy(j)
        dk, dv = cache_block(yt * 2 + c)
        copy.wait_recv()
        cache[yt, c, :, 0:128] = (dk + cache_pair[yt, :, 0:128].astype(F32)).astype(BF)
        cache[yt, c, :, 128:256] = (dv + cache_pair[yt, :, 128:256].astype(F32)).astype(BF)
        return 0

    lax.fori_loop(0, 4, cache_theirs, 0)
    lax.fori_loop(0, 4, cache_ours, 0)
    cring = Ring(
        "y", NY, y, lambda b, h: cache.at[b, c, pl.ds(h * 256, 256)], cache_land, sems, GATHER + 14
    )
    cring.step(0)
    at_ref[...] = atf[...].astype(BF)
    dt_ref[256:384, :] = dqf[...].astype(BF)
    d_ref[:, 256:384] = dqf[...].T.astype(BF)
    cring.step(1)

    def cache_out(half, total):
        d_ref[half * 256 : half * 256 + 256, 0:256] = total.astype(BF)
        dt_ref[0:256, half * 256 : half * 256 + 256] = total.T.astype(BF)

    cring.finish(cache_out)

    base = 10
    chunks = []
    offset = 0
    for n, (kind, width) in enumerate(CHUNKS):
        part, land1, mid, land2 = bufs[4 * n : 4 * n + 4]
        wide = width // 2
        if kind == "x":
            first = Ring("x", NX, x, lambda b, h, part=part: part.at[pl.ds(h * 4, 4), b], land1, sems, base)
            second = Ring(
                "z", NZ, z, lambda b, h, mid=mid, wide=wide: mid.at[b, :, pl.ds(h * wide, wide)],
                land2, sems, base + first.count,
            )
        else:
            first = Ring("z", NZ, z, lambda b, h, part=part: part.at[b, pl.ds(h * 2, 2)], land1, sems, base)
            second = Ring(
                "x", NX, x, lambda b, h, mid=mid, wide=wide: mid.at[b, :, pl.ds(h * wide, wide)],
                land2, sems, base + first.count,
            )
        base += first.count + second.count
        chunks.append((kind, width, offset, part, mid, first, second))
        offset += width

    def token_part(n):
        kind, width, at, part, mid, first, second = chunks[n]

        def piece(i, _):
            cols = pl.multiple_of(i * 256, 256)
            got = dot_nt(d_ref[...], wcat[pl.ds(pl.multiple_of(at + cols, 256), 256), :])
            part[:, :, :, pl.ds(cols, 256)] = got.astype(BF).reshape(NZ, NX, 16, 256)
            return 0

        lax.fori_loop(0, width // 256, piece, 0)

    def middle(n):
        kind, width, at, part, mid, first, second = chunks[n]
        count = 4 if kind == "x" else 2

        def write(half, total):
            mid[pl.ds(half * count, count)] = total.astype(BF)

        first.finish(write)

    def end(n):
        kind, width, at, part, mid, first, second = chunks[n]

        def write(half, total):
            tg_ref[:, pl.ds(at + half * (width // 2), width // 2)] = total.astype(BF)

        second.finish(write)

    def weight_block(yt, ct):
        cols = pl.ds(pl.multiple_of((yt * 2 + ct) * 640, 128), 640)
        top = jnp.dot(dt_ref[...], tokens[:, cols], preferred_element_type=F32)
        low = jnp.dot(at_ref[...], outg[:, cols], preferred_element_type=F32)
        return top, low

    def pair_copy(j):
        yt = turn(y, 2 + 3 * j, NY)
        return yt, pltpu.make_async_remote_copy(
            src_ref=wp.at[yt, 1 - c], dst_ref=pair_land.at[yt],
            send_sem=send_sem.at[j], recv_sem=recv_sem.at[j],
            device_id=peer_on("c", 1), device_id_type=MESH,
        )

    def theirs(j, _):
        yt, copy = pair_copy(j)
        top, low = weight_block(yt, 1 - c)
        wp[yt, 1 - c, 0:384, :] = top.astype(BF)
        wp[yt, 1 - c, 384:512, :] = low.astype(BF)
        copy.start()
        return 0

    def ours(j, _):
        yt, copy = pair_copy(j)
        top, low = weight_block(yt, c)
        copy.wait_recv()
        wp[yt, c, 0:384, :] = (top + pair_land[yt, 0:384, :].astype(F32)).astype(BF)
        wp[yt, c, 384:512, :] = (low + pair_land[yt, 384:512, :].astype(F32)).astype(BF)
        return 0

    yring = Ring("y", NY, y, lambda b, h: wp.at[b, c, pl.ds(h * 256, 256)], y_land, sems, 4)

    firsts = [chunk[5] for chunk in chunks]
    seconds = [chunk[6] for chunk in chunks]
    token_part(0)
    firsts[0].step(0)
    token_part(1)
    firsts[1].step(0)
    lax.fori_loop(0, 4, theirs, 0)
    token_part(2)
    firsts[2].step(0)
    token_part(3)
    firsts[3].step(0)
    lax.fori_loop(0, 4, ours, 0)
    yring.step(0)
    firsts[0].step(1)
    token_part(4)
    firsts[1].step(1)
    firsts[4].step(0)
    firsts[3].step(1)
    firsts[2].step(1)
    yring.step(1)
    firsts[1].step(2)
    middle(0)
    seconds[0].step(0)
    firsts[3].step(2)
    firsts[4].step(1)
    seconds[0].step(1)
    firsts[1].step(3)
    seconds[0].step(2)
    firsts[3].step(3)
    middle(2)
    seconds[2].step(0)
    seconds[0].step(3)
    middle(1)
    seconds[1].step(0)
    seconds[2].step(1)
    middle(3)
    seconds[3].step(0)
    middle(4)
    seconds[4].step(0)
    seconds[1].step(1)
    seconds[2].step(2)
    seconds[4].step(1)
    seconds[3].step(1)
    seconds[2].step(3)
    seconds[4].step(2)
    end(0)
    end(1)

    def weights_out(half, total):
        if half == 0:
            kg_ref[...] = total[0:128].T.astype(BF)
            vg_ref[...] = total[128:256].T.astype(BF)
        else:
            qg_ref[...] = total[0:128].T.astype(BF)
            og_ref[...] = total[128:256].astype(BF)

    yring.finish(weights_out)
    seconds[4].step(3)
    end(3)
    end(2)
    end(4)
    for j in range(4):
        pair_copy(j)[1].wait_send()
    for copy in near + far + across:
        copy.wait_send()
    for j in range(4):
        cache_copy(j)[1].wait_send()
    cring.drain()
    yring.drain()
    for ring in firsts + seconds:
        ring.drain()


def local(tokens, w_query, w_key, w_value, w_out, out_grad, frame_lists):
    bufs = []
    for kind, width in CHUNKS:
        bufs.append(pltpu.VMEM((NZ, NX, 16, width), BF))
        if kind == "x":
            bufs += [
                pltpu.VMEM((6, 4, 16, width), BF), pltpu.VMEM((NZ, 16, width), BF),
                pltpu.VMEM((14, 16, width // 2), BF),
            ]
        else:
            bufs += [
                pltpu.VMEM((14, 2, 16, width), BF), pltpu.VMEM((NX, 16, width), BF),
                pltpu.VMEM((6, 16, width // 2), BF),
            ]
    count = GATHER + 20
    hbm = pl.BlockSpec(memory_space=pl.ANY)
    vmem = pl.BlockSpec(memory_space=pltpu.VMEM)
    return pl.pallas_call(
        grads_kernel,
        out_shape=(
            jax.ShapeDtypeStruct((16, 5120), BF),
            jax.ShapeDtypeStruct((640, 128), BF),
            jax.ShapeDtypeStruct((640, 128), BF),
            jax.ShapeDtypeStruct((640, 128), BF),
            jax.ShapeDtypeStruct((128, 640), BF),
        ),
        in_specs=[hbm] * 6 + [pl.BlockSpec(memory_space=pltpu.SMEM)],
        out_specs=[vmem] * 5,
        scratch_shapes=[
            pltpu.VMEM((512, 5120), BF),
            pltpu.VMEM((512, 5120), BF),
            pltpu.VMEM((5120, 384), BF),
            pltpu.VMEM((128, 5120), BF),
            pltpu.VMEM((8, 512, 256), BF),
            pltpu.VMEM((512, 128), BF),
            pltpu.VMEM((512, 128), BF),
            pltpu.VMEM((8, 512, 512), F32),
            pltpu.VMEM((8, 512, 512), F32),
            pltpu.VMEM((1, 512), F32),
            pltpu.VMEM((1, 512), F32),
            pltpu.VMEM((1, 512), F32),
            pltpu.VMEM((128, 512), F32),
            pltpu.VMEM((128, 512), F32),
            pltpu.VMEM((NY, 2, 512, 256), BF),
            pltpu.VMEM((NY, 512, 256), BF),
            pltpu.VMEM((6, 256, 256), BF),
            pltpu.VMEM((512, 384), BF),
            pltpu.VMEM((384, 512), BF),
            pltpu.VMEM((128, 512), BF),
            pltpu.VMEM((NY, 2, 512, 640), BF),
            pltpu.VMEM((NY, 512, 640), BF),
            pltpu.VMEM((6, 256, 640), BF),
            pltpu.SemaphoreType.DMA((6,)),
            pltpu.SemaphoreType.DMA((count,)),
            pltpu.SemaphoreType.DMA((count,)),
        ] + bufs,
        compiler_params=pltpu.CompilerParams(
            collective_id=1, has_side_effects=True, vmem_limit_bytes=67_000_000
        ),
    )(tokens, out_grad, w_key, w_value, w_query, w_out, frame_lists)


def solution(mesh):
    in_specs = (
        P("tm", None),
        P(None, "head"),
        P(None, "head"),
        P(None, "head"),
        P("head", None),
        P("tm", None),
        P(),
    )
    out_specs = (
        P(("tm", "head"), None),
        P("tm", "head"),
        P("tm", "head"),
        P("tm", "head"),
        P("head", "tm"),
    )
    return jax.shard_map(local, mesh=mesh, in_specs=in_specs, out_specs=out_specs, check_vma=False)
```

```python
import jax
import jax.numpy as jnp
from jax import lax
from jax.experimental import pallas as pl
from jax.experimental.pallas import tpu as pltpu
from jax.sharding import PartitionSpec as P

MESH = pl.DeviceIdType.MESH
BF = jnp.bfloat16
F32 = jnp.float32
CHUNKS = (("x", 1024), ("z", 1024), ("x", 1024), ("z", 1024), ("x", 1024))
NX, NY, NZ = 4, 4, 8
ORDER = sum(j << 2 * i for i, j in enumerate((0, 1, 0, 3, 1, 3, 2, 2)))
OURS = sum(1 << i for i in (2, 4, 5, 7))
GATHER = 10 + 20 * len(CHUNKS)


def dot_nt(left, right):
    return lax.dot_general(left, right, (((1,), (1,)), ((), ())), preferred_element_type=F32)


def dot_tn(left, right):
    return lax.dot_general(left, right, (((0,), (0,)), ((), ())), preferred_element_type=F32)


def place():
    t, h = lax.axis_index("tm"), lax.axis_index("head")
    return lax.div(t, 2), lax.rem(t, 2), lax.div(h, NX), lax.rem(h, NX)


def device(y, c, z, x):
    return (y * 2 + c, z * NX + x)


def turn(at, by, n):
    return lax.rem(at + by + n, n)


def peer_on(axis, step):
    y, c, z, x = place()
    if axis == "x":
        return device(y, c, z, turn(x, step, NX))
    if axis == "y":
        return device(turn(y, step, NY), c, z, x)
    if axis == "z":
        return device(y, c, turn(z, step, NZ), x)
    return device(y, 1 - c, z, x)


class Ring:
    def __init__(self, axis, n, me, own, land, sems, base):
        self.axis, self.n, self.me, self.own, self.land = axis, n, me, own, land
        self.send, self.recv = sems
        self.ids, count = {}, 0
        for p in range(n // 2):
            for way, half in ((0, 0), (1, 1), (0, 1), (1, 0)):
                if p < self.length(way, half):
                    self.ids[way, half, p] = count
                    count += 1
        self.base = base
        self.count = count

    def length(self, way, half):
        return self.n // 2 if way == half else self.n // 2 - 1

    def copy(self, way, half, p):
        step = (-1, 1)[way]
        target = turn(self.me, step * (self.length(way, half) - p), self.n)
        i = self.ids[way, half, p]
        return target, pltpu.make_async_remote_copy(
            src_ref=self.own(target, half),
            dst_ref=self.land.at[i],
            send_sem=self.send.at[self.base + i],
            recv_sem=self.recv.at[self.base + i],
            device_id=peer_on(self.axis, step),
            device_id_type=MESH,
        )

    def step(self, p):
        for way, half in ((0, 0), (1, 1), (0, 1), (1, 0)):
            if p >= self.length(way, half):
                continue
            target, copy = self.copy(way, half, p)
            if p > 0:
                self.copy(way, half, p - 1)[1].wait_recv()
                mine = self.own(target, half)
                mine[...] = mine[...] + self.land[self.ids[way, half, p - 1]]
            copy.start()

    def finish(self, write):
        for half in (0, 1):
            total = self.own(self.me, half)[...].astype(F32)
            for way in (0, 1):
                last = self.length(way, half) - 1
                self.copy(way, half, last)[1].wait_recv()
                total = total + self.land[self.ids[way, half, last]].astype(F32)
            write(half, total)

    def drain(self):
        for way, half, p in self.ids:
            self.copy(way, half, p)[1].wait_send()


def greet(axes):
    barrier = pltpu.get_barrier_semaphore()
    peers = []
    for axis in axes:
        peers += [peer_on(axis, 1)] if axis == "c" else [peer_on(axis, -1), peer_on(axis, 1)]
    for peer in peers:
        pl.semaphore_signal(barrier, inc=1, device_id=peer, device_id_type=MESH)
    pl.semaphore_wait(barrier, len(peers))


def grads_kernel(
    tokens_hbm, outg_hbm, wk_hbm, wv_hbm, wq_hbm, wo_hbm, lists_ref,
    tg_ref, qg_ref, kg_ref, vg_ref, og_ref,
    tokens, outg, wcat, wout, kv, query, d_attn, scores, dprobs, top_ref, sum_ref, del_ref, atf, dqf,
    cache, cache_pair, cache_land, d_ref, dt_ref, at_ref,
    wp, pair_land, y_land, in_sem, send_sem, recv_sem, *bufs
):
    y, c, z, x = place()
    sems = (send_sem, recv_sem)
    me = y * 2 + c
    scale = 1.0 / 128**0.5
    loads = [
        pltpu.make_async_copy(src, dst, in_sem.at[i])
        for i, (src, dst) in enumerate((
            (wk_hbm, wcat.at[:, pl.ds(0, 128)]), (wv_hbm, wcat.at[:, pl.ds(128, 128)]), (tokens_hbm, tokens),
            (wq_hbm, wcat.at[:, pl.ds(256, 128)]), (outg_hbm, outg), (wo_hbm, wout),
        ))
    ]
    for load in loads:
        load.start()

    def block(dy, core):
        return turn(y, dy, NY) * 2 + core

    def move(i, blk, rows, axis, step):
        ref = kv.at[blk, rows]
        return pltpu.make_async_remote_copy(
            src_ref=ref, dst_ref=ref,
            send_sem=send_sem.at[GATHER + i], recv_sem=recv_sem.at[GATHER + i],
            device_id=peer_on(axis, step), device_id_type=MESH,
        )

    low, high, whole = pl.ds(0, 256), pl.ds(256, 256), pl.ds(0, 512)
    near = [
        move(0, me, low, "y", 1), move(3, me, high, "y", -1),
        move(1, me, high, "y", 1), move(2, me, low, "y", -1),
    ]
    far = [move(4, block(3, c), low, "y", 1), move(5, block(1, c), high, "y", -1)]
    across = [move(6 + dy, block(dy, c), whole, "c", 1) for dy in range(4)]

    def span(k):
        return pl.ds(pl.multiple_of(k * 640, 128), 640)

    def project_kv(k, _):
        scores[0, :, 0:256] += jnp.dot(tokens[:, span(k)], wcat[span(k), 0:256], preferred_element_type=F32)
        return 0

    def project_rest(k, _):
        scores[0, :, 0:128] += jnp.dot(tokens[:, span(k)], wcat[span(k), 256:384], preferred_element_type=F32)
        scores[0, :, 128:256] += dot_nt(outg[:, span(k)], wout[:, span(k)])
        return 0

    greet(("x", "z", "y", "c"))
    scores[0] = jnp.zeros((512, 512), F32)
    for load in loads[:3]:
        load.wait()
    lax.fori_loop(0, 8, project_kv, 0)
    kv[me] = scores[0, :, 0:256].astype(BF)
    for copy in near:
        copy.start()
    across[0].start()
    scores[0] = jnp.zeros((512, 512), F32)
    for load in loads[3:]:
        load.wait()
    lax.fori_loop(0, 8, project_rest, 0)
    query[...] = scores[0, :, 0:128].astype(BF)
    d_attn[...] = scores[0, :, 128:256].astype(BF)
    top_ref[...] = jnp.full((1, 512), -3e30, F32)
    sum_ref[...] = jnp.zeros((1, 512), F32)
    del_ref[...] = jnp.zeros((1, 512), F32)
    atf[...] = jnp.zeros((128, 512), F32)
    dqf[...] = jnp.zeros((128, 512), F32)

    def score(i, _):
        pair, other = lax.div(i, 2), lax.rem(i, 2)
        dy = jnp.where(pair == 1, 3, jnp.where(pair == 2, 1, jnp.where(pair == 3, 2, 0)))
        b = block(dy, jnp.where(other == 1, 1 - c, c))

        @pl.when(i == 1)
        def _():
            across[0].wait_recv()

        @pl.when(i == 2)
        def _():
            near[0].wait_recv()
            far[0].start()
            near[1].wait_recv()
            far[1].start()
            near[2].wait_recv()
            across[3].start()
            near[3].wait_recv()
            across[1].start()

        @pl.when(i == 3)
        def _():
            across[3].wait_recv()

        @pl.when(i == 5)
        def _():
            across[1].wait_recv()

        @pl.when(i == 6)
        def _():
            far[0].wait_recv()
            far[1].wait_recv()
            across[2].start()

        @pl.when(i == 7)
        def _():
            across[2].wait_recv()

        seen = (b == me) | ((b < me) & (lists_ref[me, b] == 1))
        shut = jnp.where(seen, 0.0, -1e30).astype(F32)
        got = dot_nt(kv[b, :, 0:128], query[...]) * scale + shut
        scores[b] = got
        top_ref[...] = jnp.maximum(top_ref[...], jnp.max(got, axis=0, keepdims=True))
        dprobs[b] = dot_nt(kv[b, :, 128:256], d_attn[...])
        return 0

    lax.fori_loop(0, 8, score, 0)

    def weigh(b, _):
        got = jnp.exp(scores[b] - top_ref[...])
        scores[b] = got
        sum_ref[...] += jnp.sum(got, axis=0, keepdims=True)
        del_ref[...] += jnp.sum(got * dprobs[b], axis=0, keepdims=True)
        return 0

    lax.fori_loop(0, 8, weigh, 0)
    sum_ref[...] = 1.0 / sum_ref[...]
    del_ref[...] = del_ref[...] * sum_ref[...]

    def cache_block(b):
        probs = scores[b] * sum_ref[...]
        probs_b = probs.astype(BF)
        dscore = (probs * (dprobs[b] - del_ref[...]) * scale).astype(BF)
        atf[...] += dot_tn(kv[b, :, 128:256], probs_b)
        dqf[...] += dot_tn(kv[b, :, 0:128], dscore)
        dk = jnp.dot(dscore, query[...], preferred_element_type=F32)
        dv = jnp.dot(probs_b, d_attn[...], preferred_element_type=F32)
        return dk, dv

    def cache_copy(j):
        yt = turn(y, 2 + 3 * j, NY)
        return yt, pltpu.make_async_remote_copy(
            src_ref=cache.at[yt, 1 - c], dst_ref=cache_pair.at[yt],
            send_sem=send_sem.at[GATHER + 10 + j], recv_sem=recv_sem.at[GATHER + 10 + j],
            device_id=peer_on("c", 1), device_id_type=MESH,
        )

    cring = Ring(
        "y", NY, y, lambda b, h: cache.at[b, c, pl.ds(h * 256, 256)], cache_land, sems, GATHER + 14
    )

    def cache_step(i, _):
        j = lax.shift_right_logical(jnp.int32(ORDER), 2 * i) & 3
        ours = (lax.shift_right_logical(jnp.int32(OURS), i) & 1) == 1
        yt, copy = cache_copy(j)
        dk, dv = cache_block(yt * 2 + jnp.where(ours, c, 1 - c))

        @pl.when(jnp.logical_not(ours))
        def _():
            cache[yt, 1 - c, :, 0:128] = dk.astype(BF)
            cache[yt, 1 - c, :, 128:256] = dv.astype(BF)
            copy.start()

        @pl.when(ours)
        def _():
            copy.wait_recv()
            cache[yt, c, :, 0:128] = (dk + cache_pair[yt, :, 0:128].astype(F32)).astype(BF)
            cache[yt, c, :, 128:256] = (dv + cache_pair[yt, :, 128:256].astype(F32)).astype(BF)

        @pl.when(i == 2)
        def _():
            cring.copy(0, 0, 0)[1].start()
            cring.copy(1, 1, 0)[1].start()

        @pl.when(i == 4)
        def _():
            cring.copy(1, 0, 0)[1].start()

        @pl.when(i == 5)
        def _():
            cring.copy(0, 1, 0)[1].start()

        @pl.when(i == 6)
        def _():
            cring.step(1)

        return 0

    lax.fori_loop(0, 8, cache_step, 0)
    at_ref[...] = atf[...].astype(BF)
    dt_ref[256:384, :] = dqf[...].astype(BF)
    d_ref[:, 256:384] = dqf[...].T.astype(BF)

    def early(i, _):
        cols = pl.ds(pl.multiple_of(i * 640, 128), 640)
        yt, ct = lax.div(i, 2), lax.rem(i, 2)
        wp[yt, ct, 256:384, :] = jnp.dot(dt_ref[256:384, :], tokens[:, cols], preferred_element_type=F32).astype(BF)
        wp[yt, ct, 384:512, :] = jnp.dot(at_ref[...], outg[:, cols], preferred_element_type=F32).astype(BF)
        return 0

    lax.fori_loop(0, 8, early, 0)

    def cache_out(half, total):
        d_ref[half * 256 : half * 256 + 256, 0:256] = total.astype(BF)
        dt_ref[0:256, half * 256 : half * 256 + 256] = total.T.astype(BF)

    cring.finish(cache_out)

    base = 10
    chunks = []
    offset = 0
    for n, (kind, width) in enumerate(CHUNKS):
        part, land1, mid, land2 = bufs[4 * n : 4 * n + 4]
        wide = width // 2
        if kind == "x":
            first = Ring("x", NX, x, lambda b, h, part=part: part.at[pl.ds(h * 4, 4), b], land1, sems, base)
            second = Ring(
                "z", NZ, z, lambda b, h, mid=mid, wide=wide: mid.at[b, :, pl.ds(h * wide, wide)],
                land2, sems, base + first.count,
            )
        else:
            first = Ring("z", NZ, z, lambda b, h, part=part: part.at[b, pl.ds(h * 2, 2)], land1, sems, base)
            second = Ring(
                "x", NX, x, lambda b, h, mid=mid, wide=wide: mid.at[b, :, pl.ds(h * wide, wide)],
                land2, sems, base + first.count,
            )
        base += first.count + second.count
        chunks.append((kind, width, offset, part, mid, first, second))
        offset += width

    def token_part(n):
        kind, width, at, part, mid, first, second = chunks[n]

        def piece(i, _):
            cols = pl.multiple_of(i * 256, 256)
            got = dot_nt(d_ref[...], wcat[pl.ds(pl.multiple_of(at + cols, 256), 256), :])
            part[:, :, :, pl.ds(cols, 256)] = got.astype(BF).reshape(NZ, NX, 16, 256)
            return 0

        lax.fori_loop(0, width // 256, piece, 0)

    def middle(n):
        kind, width, at, part, mid, first, second = chunks[n]
        count = 4 if kind == "x" else 2

        def write(half, total):
            mid[pl.ds(half * count, count)] = total.astype(BF)

        first.finish(write)

    def end(n):
        kind, width, at, part, mid, first, second = chunks[n]

        def write(half, total):
            tg_ref[:, pl.ds(at + half * (width // 2), width // 2)] = total.astype(BF)

        second.finish(write)

    def weight_block(yt, ct):
        cols = pl.ds(pl.multiple_of((yt * 2 + ct) * 640, 128), 640)
        return jnp.dot(dt_ref[0:256, :], tokens[:, cols], preferred_element_type=F32)

    def pair_copy(j):
        yt = turn(y, 2 + 3 * j, NY)
        return yt, pltpu.make_async_remote_copy(
            src_ref=wp.at[yt, 1 - c], dst_ref=pair_land.at[yt],
            send_sem=send_sem.at[j], recv_sem=recv_sem.at[j],
            device_id=peer_on("c", 1), device_id_type=MESH,
        )

    def theirs(j, _):
        yt, copy = pair_copy(j)
        wp[yt, 1 - c, 0:256, :] = weight_block(yt, 1 - c).astype(BF)
        copy.start()
        return 0

    def ours(j, _):
        yt, copy = pair_copy(j)
        top = weight_block(yt, c)
        copy.wait_recv()
        wp[yt, c, 0:256, :] = (top + pair_land[yt, 0:256, :].astype(F32)).astype(BF)
        wp[yt, c, 256:512, :] = wp[yt, c, 256:512, :] + pair_land[yt, 256:512, :]
        return 0

    yring = Ring("y", NY, y, lambda b, h: wp.at[b, c, pl.ds(h * 256, 256)], y_land, sems, 4)

    firsts = [chunk[5] for chunk in chunks]
    seconds = [chunk[6] for chunk in chunks]
    token_part(0)
    firsts[0].step(0)
    token_part(1)
    firsts[1].step(0)
    lax.fori_loop(0, 4, theirs, 0)
    token_part(2)
    firsts[2].step(0)
    token_part(3)
    firsts[3].step(0)
    lax.fori_loop(0, 4, ours, 0)
    yring.step(0)
    firsts[0].step(1)
    token_part(4)
    firsts[1].step(1)
    firsts[4].step(0)
    firsts[3].step(1)
    firsts[2].step(1)
    yring.step(1)
    firsts[1].step(2)
    middle(0)
    seconds[0].step(0)
    firsts[3].step(2)
    firsts[4].step(1)
    seconds[0].step(1)
    firsts[1].step(3)
    seconds[0].step(2)
    firsts[3].step(3)
    middle(2)
    seconds[2].step(0)
    seconds[0].step(3)
    middle(1)
    seconds[1].step(0)
    seconds[2].step(1)
    middle(3)
    seconds[3].step(0)
    middle(4)
    seconds[4].step(0)
    seconds[1].step(1)
    seconds[2].step(2)
    seconds[4].step(1)
    seconds[3].step(1)
    seconds[2].step(3)
    seconds[4].step(2)
    end(0)
    end(1)

    def weights_out(half, total):
        if half == 0:
            kg_ref[...] = total[0:128].T.astype(BF)
            vg_ref[...] = total[128:256].T.astype(BF)
        else:
            qg_ref[...] = total[0:128].T.astype(BF)
            og_ref[...] = total[128:256].astype(BF)

    yring.finish(weights_out)
    seconds[4].step(3)
    end(3)
    end(2)
    end(4)
    for j in range(4):
        pair_copy(j)[1].wait_send()
    for copy in near + far + across:
        copy.wait_send()
    for j in range(4):
        cache_copy(j)[1].wait_send()
    cring.drain()
    yring.drain()
    for ring in firsts + seconds:
        ring.drain()


def local(tokens, w_query, w_key, w_value, w_out, out_grad, frame_lists):
    bufs = []
    for kind, width in CHUNKS:
        bufs.append(pltpu.VMEM((NZ, NX, 16, width), BF))
        if kind == "x":
            bufs += [
                pltpu.VMEM((6, 4, 16, width), BF), pltpu.VMEM((NZ, 16, width), BF),
                pltpu.VMEM((14, 16, width // 2), BF),
            ]
        else:
            bufs += [
                pltpu.VMEM((14, 2, 16, width), BF), pltpu.VMEM((NX, 16, width), BF),
                pltpu.VMEM((6, 16, width // 2), BF),
            ]
    count = GATHER + 20
    hbm = pl.BlockSpec(memory_space=pl.ANY)
    vmem = pl.BlockSpec(memory_space=pltpu.VMEM)
    return pl.pallas_call(
        grads_kernel,
        out_shape=(
            jax.ShapeDtypeStruct((16, 5120), BF),
            jax.ShapeDtypeStruct((640, 128), BF),
            jax.ShapeDtypeStruct((640, 128), BF),
            jax.ShapeDtypeStruct((640, 128), BF),
            jax.ShapeDtypeStruct((128, 640), BF),
        ),
        in_specs=[hbm] * 6 + [pl.BlockSpec(memory_space=pltpu.SMEM)],
        out_specs=[vmem] * 5,
        scratch_shapes=[
            pltpu.VMEM((512, 5120), BF),
            pltpu.VMEM((512, 5120), BF),
            pltpu.VMEM((5120, 384), BF),
            pltpu.VMEM((128, 5120), BF),
            pltpu.VMEM((8, 512, 256), BF),
            pltpu.VMEM((512, 128), BF),
            pltpu.VMEM((512, 128), BF),
            pltpu.VMEM((8, 512, 512), F32),
            pltpu.VMEM((8, 512, 512), F32),
            pltpu.VMEM((1, 512), F32),
            pltpu.VMEM((1, 512), F32),
            pltpu.VMEM((1, 512), F32),
            pltpu.VMEM((128, 512), F32),
            pltpu.VMEM((128, 512), F32),
            pltpu.VMEM((NY, 2, 512, 256), BF),
            pltpu.VMEM((NY, 512, 256), BF),
            pltpu.VMEM((6, 256, 256), BF),
            pltpu.VMEM((512, 384), BF),
            pltpu.VMEM((384, 512), BF),
            pltpu.VMEM((128, 512), BF),
            pltpu.VMEM((NY, 2, 512, 640), BF),
            pltpu.VMEM((NY, 512, 640), BF),
            pltpu.VMEM((6, 256, 640), BF),
            pltpu.SemaphoreType.DMA((6,)),
            pltpu.SemaphoreType.DMA((count,)),
            pltpu.SemaphoreType.DMA((count,)),
        ] + bufs,
        compiler_params=pltpu.CompilerParams(
            collective_id=1, has_side_effects=True, vmem_limit_bytes=67_000_000
        ),
    )(tokens, out_grad, w_key, w_value, w_query, w_out, frame_lists)


def solution(mesh):
    in_specs = (
        P("tm", None),
        P(None, "head"),
        P(None, "head"),
        P(None, "head"),
        P("head", None),
        P("tm", None),
        P(),
    )
    out_specs = (
        P(("tm", "head"), None),
        P("tm", "head"),
        P("tm", "head"),
        P("tm", "head"),
        P("head", "tm"),
    )
    return jax.shard_map(local, mesh=mesh, in_specs=in_specs, out_specs=out_specs, check_vma=False)
```
